256 devices in a mesh: node: 32 (over y, x, z_lo), local: 8 (over z_hi, core).
Axes of the slice: x: 4, y: 4, z: 8 (z_hi: 4, z_lo: 2; z = z_hi * 2 + z_lo), core: 2. Of those that a mesh axis runs over, the one named last changes fastest.
Arguments:
- tokens: bfloat16 [16384, 5120], P('node', 'local'), may hold values from -6 to 6
- queries: bfloat16 [16384, 8192], P('node', 'local'), may hold values from -6 to 6
- key_weight: bfloat16 [5120, 1024], P('node', 'local'), may hold values from -0.078125 to 0.078125
- value_weight: bfloat16 [5120, 1024], P('node', 'local'), may hold values from -0.078125 to 0.078125
- query_gain: float32 [128], replicated, may hold values from 0.5 to 1.6
- key_gain: float32 [128], replicated, may hold values from 0.5 to 1.6
- segment_ids: int32 [32, 512], P('node'), may hold values from 0 to 255, never falling along the last dimension, each value on 1 to 256 neighbouring positions
- context_grad: bfloat16 [16384, 8192], P('node', 'local'), may hold values from -16 to 16
Outputs:
- context: bfloat16 [16384, 8192], P('node', 'local')
- token_grad: bfloat16 [16384, 5120], P('node', 'local')
- query_grad: bfloat16 [16384, 8192], P('node', 'local')
- key_weight_grad: float32 [5120, 1024], P('node', 'local')
- value_weight_grad: float32 [5120, 1024], P('node', 'local')
- gain_grads: float32 [2, 128], replicated
The draws below stay inside these ranges and needn't reach their ends.
Inputs may be any that keep to these rules, and one draw needn't show every extreme that they name: `segment_ids`: within each row the numbers never fall; a document is a run of equal numbers of at most half of 512 tokens.
All inputs are finite; a program needn't handle non-finite values.
Results may differ from the reference program's by a relative error of at most 0.014.
Values may be sent and summed in bfloat16 or wider, within the bound.
No kernel may reach another device: no remote copies, remote signals or barrier semaphores. Data moves between devices by JAX's collectives and lax.ppermute only.
A program may use at most 128 MiB of HBM per device.

```python
import math
import jax
import jax.numpy as jnp
import numpy as np
from jax import lax

D = 5120
HEAD = 128
KV_HEADS = 8
Q_HEADS = 64
SEQ = 512
GROUP = 8
KV_DEV = 1
TOKENS = 16384
N_LOCAL = 8


def draw_context_grad(key, part):
    row_ramp = jnp.arange(TOKENS, dtype=jnp.float32) / TOKENS
    noise = jnp.clip(jax.random.normal(key, (TOKENS, Q_HEADS * HEAD), jnp.float32), -5.0, 5.0)
    row_scale = 1.0 + 2.0 * row_ramp
    return (noise * row_scale[:, None]).astype(jnp.bfloat16)


def steps_of(stream_key, shape, pieces, least, largest):
    level, own = 1.0, jax.random.fold_in(stream_key, 6)
    for dim, blocks in pieces:
        steps = jnp.exp(jax.random.uniform(jax.random.fold_in(own, dim), (blocks,), jnp.float32, least / len(pieces), largest / len(pieces)))
        level = level * jnp.repeat(steps, shape[dim] // blocks).reshape([-1 if axis == dim else 1 for axis in range(len(shape))])
    return level


def split_up(count, total, most, slope):
    portions = [(1 << 20) // math.isqrt(standing ** slope) + 1 for standing in range(2, count + 1)]
    rest, holding = total - most - (count - 1), [1] * (count - 1)
    while rest > 0:
        movable = [i for i in range(count - 1) if holding[i] < most]
        pool, left = sum([portions[i] for i in movable]), rest
        for i in movable:
            extra = min(most - holding[i], max(1, left * portions[i] // pool), rest)
            holding[i] = holding[i] + extra
            rest = rest - extra
    return np.array([most] + holding)


def ragged(own_key, amount, total, reach, slope):
    if amount == 2:
        one = jax.random.randint(own_key, (), max(1, total - reach), min(reach, total - 1) + 1)
        return jnp.stack([one, total - one])
    sizes = jnp.asarray(split_up(amount, total, reach, slope), jnp.int32)
    twos = (amount - 1) // 2
    source_of, receiver = sizes[1:1 + 2 * twos:2], sizes[2:2 + 2 * twos:2]
    margin = jnp.minimum(source_of - 1, reach - receiver)
    passed = jax.random.randint(jax.random.fold_in(own_key, 1), (twos,), 0, 1 << 20) % (margin + 1)
    sizes = sizes.at[1:1 + 2 * twos:2].set(source_of - passed).at[2:2 + 2 * twos:2].set(receiver + passed)
    return sizes[jax.random.permutation(jax.random.fold_in(own_key, 2), amount)]


def bell_draw(stream_key, extent, deviation, reach, split=(), held_as=jnp.bfloat16):
    values = jax.random.normal(stream_key, extent, jnp.float32) * deviation
    if len(split) > 0:
        values = steps_of(stream_key, extent, split, -0.22, 0.18) * values
    return jnp.clip(values, min=-reach, max=reach).astype(held_as)


def setup_inputs(seed: int = 0) -> dict:
    splits = jax.random.split(jax.random.key(seed), 9)
    return {
        "tokens": bell_draw(splits[0], (TOKENS, D), 1.0, 6.0, ((0, 32), (1, 8))),
        "queries": bell_draw(splits[1], (TOKENS, Q_HEADS * HEAD), 1.0, 6.0, ((0, 32), (1, 8))),
        "key_weight": bell_draw(splits[2], (D, KV_HEADS * HEAD), D ** -0.5, 0.078125, ((0, 32), (1, 8))),
        "value_weight": bell_draw(splits[3], (D, KV_HEADS * HEAD), D ** -0.5, 0.078125, ((0, 32), (1, 8))),
        "query_gain": jnp.clip(jnp.exp(jax.random.uniform(splits[4], (HEAD,), jnp.float32, math.log(0.5), math.log(1.6))), 0.5, 1.6),
        "key_gain": jnp.clip(jnp.exp(jax.random.uniform(splits[5], (HEAD,), jnp.float32, math.log(0.5), math.log(1.6))), 0.5, 1.6),
        "segment_ids": jax.vmap(lambda own: jnp.searchsorted(jnp.cumsum(ragged(own, SEQ // 2, SEQ, SEQ // 2, 2)), jnp.arange(SEQ), side="right"))(jax.random.split(splits[6], (TOKENS // SEQ))).reshape((TOKENS // SEQ, SEQ)).astype(jnp.int32),
        "context_grad": draw_context_grad(jax.random.fold_in(splits[8], 71), 0),
    }


EPS = 1e-06
THETA = 1000000.0

def rope_tables(segments, head_size):
    length = segments.shape[0]
    token_index = jnp.arange(length, dtype=jnp.int32)
    starts = jnp.concatenate([jnp.ones((1,), dtype=bool), segments[1:] != segments[:-1]])
    run_first = lax.cummax(jnp.where(starts, token_index, 0).astype(jnp.int32), axis=0)
    position = (token_index - run_first).astype(jnp.float32)
    frequency = THETA ** (-2.0 * jnp.arange(head_size // 2, dtype=jnp.float32) / head_size)
    angles = position[:, None] * frequency[None, :]
    return (jnp.cos(angles), jnp.sin(angles))

def rotate(values, cosine_table, sine_table):
    half_size = values.shape[-1] // 2
    first_half = values[..., :half_size]
    second_half = values[..., half_size:]
    cos_wide = cosine_table[:, None, :]
    sin_wide = sine_table[:, None, :]
    return jnp.concatenate([first_half * cos_wide - second_half * sin_wide, second_half * cos_wide + first_half * sin_wide], axis=-1)

def rotate_back(values, cosine_table, sine_table):
    half_size = values.shape[-1] // 2
    first_half = values[..., :half_size]
    second_half = values[..., half_size:]
    cos_wide = cosine_table[:, None, :]
    sin_wide = sine_table[:, None, :]
    return jnp.concatenate([first_half * cos_wide + second_half * sin_wide, second_half * cos_wide - first_half * sin_wide], axis=-1)

def normalize(values, gain_vector):
    inverse_rms = lax.rsqrt(lax.optimization_barrier(jnp.mean(values * values, axis=-1, keepdims=True)) + EPS)
    return (values * inverse_rms * gain_vector, inverse_rms)

def normalize_back(values, inverse_rms, gain_vector, upstream):
    weighted = gain_vector * upstream
    return inverse_rms * weighted - values * inverse_rms ** 3 * lax.optimization_barrier(jnp.mean(values * weighted, axis=-1, keepdims=True))

def sequence_pass(token_seq, query_seq, grad_seq, segments, key_weight, value_weight, query_gain, key_gain):
    seq_len = token_seq.shape[0]
    score_scale = HEAD ** (-0.5)
    cosine_table, sine_table = rope_tables(segments, HEAD)
    key_raw = jnp.dot(token_seq, key_weight, preferred_element_type=jnp.float32).reshape(seq_len, KV_HEADS, HEAD)
    value_bf = jnp.dot(token_seq, value_weight, preferred_element_type=jnp.float32).astype(jnp.bfloat16).reshape(seq_len, KV_HEADS, HEAD)
    key_normed, key_scale = normalize(key_raw, key_gain)
    key_rot = rotate(key_normed, cosine_table, sine_table).astype(jnp.bfloat16)
    query_wide = query_seq.astype(jnp.float32).reshape(seq_len, Q_HEADS, HEAD)
    query_normed, query_scale = normalize(query_wide, query_gain)
    query_rot = rotate(query_normed, cosine_table, sine_table).astype(jnp.bfloat16).reshape(seq_len, KV_HEADS, GROUP, HEAD)
    grad_rows = grad_seq.reshape(seq_len, KV_HEADS, GROUP, HEAD)
    token_index = jnp.arange(seq_len, dtype=jnp.int32)
    allowed = (segments[:, None] == segments[None, :]) & (token_index[None, :] <= token_index[:, None])

    def per_head(operands):
        query_head, key_head, value_head, grad_head = operands
        query_f = query_head.astype(jnp.float32)
        key_f = key_head.astype(jnp.float32)
        value_f = value_head.astype(jnp.float32)
        grad_f = grad_head.astype(jnp.float32)
        scores = jnp.einsum('qgh,kh->gqk', query_f, key_f) * score_scale
        exponent = jnp.where(allowed[None], jnp.exp(scores), 0.0)
        weights = exponent / lax.optimization_barrier(jnp.sum(exponent, axis=-1, keepdims=True))
        rounded = weights.astype(jnp.bfloat16).astype(jnp.float32)
        context_head = jnp.einsum('gqk,kh->qgh', rounded, value_f).astype(jnp.bfloat16)
        dot_grad = jnp.einsum('qgh,kh->gqk', grad_f, value_f)
        delta_row = lax.optimization_barrier(jnp.sum(weights * dot_grad, axis=-1, keepdims=True))
        score_grad = (weights * (dot_grad - delta_row) * score_scale).astype(jnp.bfloat16).astype(jnp.float32)
        value_grad = jnp.einsum('gqk,qgh->kh', rounded, grad_f).astype(jnp.bfloat16)
        query_rot_grad = jnp.einsum('gqk,kh->qgh', score_grad, key_f)
        key_rot_grad = jnp.einsum('gqk,qgh->kh', score_grad, query_f)
        return (context_head, value_grad, query_rot_grad, key_rot_grad)
    results = lax.map(per_head, (jnp.moveaxis(query_rot, 1, 0), jnp.moveaxis(key_rot, 1, 0), jnp.moveaxis(value_bf, 1, 0), jnp.moveaxis(grad_rows, 1, 0)))
    context = jnp.moveaxis(results[0], 0, 1).reshape(seq_len, Q_HEADS * HEAD)
    value_grad = jnp.moveaxis(results[1], 0, 1).reshape(seq_len, KV_HEADS * HEAD)
    query_rot_grad = jnp.moveaxis(results[2], 0, 1).reshape(seq_len, Q_HEADS, HEAD)
    key_rot_grad = jnp.moveaxis(results[3], 0, 1)
    query_normed_grad = rotate_back(query_rot_grad, cosine_table, sine_table)
    key_normed_grad = rotate_back(key_rot_grad, cosine_table, sine_table)
    query_grad = normalize_back(query_wide, query_scale, query_gain, query_normed_grad).astype(jnp.bfloat16).reshape(seq_len, Q_HEADS * HEAD)
    key_grad = normalize_back(key_raw, key_scale, key_gain, key_normed_grad).astype(jnp.bfloat16).reshape(seq_len, KV_HEADS * HEAD)
    gain_query = lax.optimization_barrier(jnp.sum(query_normed_grad * query_wide * query_scale, axis=(0, 1)))
    gain_key = lax.optimization_barrier(jnp.sum(key_normed_grad * key_raw * key_scale, axis=(0, 1)))
    key_part = jnp.dot(token_seq.T, key_grad, preferred_element_type=jnp.float32)
    value_part = jnp.dot(token_seq.T, value_grad, preferred_element_type=jnp.float32)
    block_width = KV_DEV * HEAD
    key_grad_blocks = key_grad.reshape(seq_len, N_LOCAL, block_width).astype(jnp.float32)
    value_grad_blocks = value_grad.reshape(seq_len, N_LOCAL, block_width).astype(jnp.float32)
    key_blocks = key_weight.reshape(D, N_LOCAL, block_width).astype(jnp.float32)
    value_blocks = value_weight.reshape(D, N_LOCAL, block_width).astype(jnp.float32)
    partial_value = jnp.einsum('snc,dnc->nsd', key_grad_blocks, key_blocks) + jnp.einsum('snc,dnc->nsd', value_grad_blocks, value_blocks)
    partial_bf = lax.optimization_barrier(partial_value.astype(jnp.bfloat16))
    token_grad = lax.optimization_barrier(jnp.sum(partial_bf.astype(jnp.float32), axis=0)).astype(jnp.bfloat16)
    return (context, token_grad, query_grad, key_part, value_part, jnp.stack([gain_query, gain_key]))

def reference(tokens, queries, key_weight, value_weight, query_gain, key_gain, segment_ids, context_grad):
    count_seq = segment_ids.shape[0]
    seq_len = segment_ids.shape[1]

    def step(totals, operands):
        token_seq, query_seq, grad_seq, segments = operands
        results = sequence_pass(token_seq, query_seq, grad_seq, segments, key_weight, value_weight, query_gain, key_gain)
        updated = (totals[0] + results[3], totals[1] + results[4], totals[2] + results[5])
        return (updated, (results[0], results[1], results[2]))
    initial = (jnp.zeros(key_weight.shape, jnp.float32), jnp.zeros(value_weight.shape, jnp.float32), jnp.zeros((2, HEAD), jnp.float32))
    operands = (tokens.reshape(count_seq, seq_len, D), queries.reshape(count_seq, seq_len, Q_HEADS * HEAD), context_grad.reshape(count_seq, seq_len, Q_HEADS * HEAD), segment_ids)
    totals, stacked = lax.scan(step, initial, operands)
    context = stacked[0].reshape(TOKENS, Q_HEADS * HEAD)
    token_grad = stacked[1].reshape(TOKENS, D)
    query_grad = stacked[2].reshape(TOKENS, Q_HEADS * HEAD)
    return (context, token_grad, query_grad, totals[0], totals[1], totals[2])
```

```python
import jax
import jax.numpy as jnp
from jax import lax
from jax.experimental import pallas as pl
from jax.experimental.pallas import tpu as pltpu
from jax.sharding import PartitionSpec as P

EPS = 1e-06
THETA = 1000000.0
AXES = ("node", "local")
F32 = jnp.float32
BF16 = jnp.bfloat16
NT = (((1,), (1,)), ((), ()))
TN = (((0,), (0,)), ((), ()))


def device(y, x, zl, zh, c):
    return (((y % 4) * 4 + x % 4) * 2 + zl % 2) * 8 + (zh % 4) * 2 + c % 2


def send(value, target):
    pairs = [
        (device(y, x, zl, zh, c), device(*target(y, x, zl, zh, c)))
        for y in range(4)
        for x in range(4)
        for zl in range(2)
        for zh in range(4)
        for c in range(2)
    ]
    return lax.ppermute(value, AXES, pairs)


def shift(value, dy=0, dx=0, dzl=0, dzh=0, dc=0):
    return send(value, lambda y, x, zl, zh, c: (y + dy, x + dx, zl + dzl, zh + dzh, c + dc))


def ring(value, axis):
    return [value] + [shift(value, **{axis: -step}) for step in (1, 2, 3)]


def rope_tables(segments, head_size):
    length = segments.shape[0]
    token_index = jnp.arange(length, dtype=jnp.int32)
    starts = jnp.concatenate([jnp.ones((1,), dtype=bool), segments[1:] != segments[:-1]])
    run_first = lax.cummax(jnp.where(starts, token_index, 0), axis=0)
    position = (token_index - run_first).astype(jnp.float32)
    frequency = THETA ** (-2.0 * jnp.arange(head_size // 2, dtype=jnp.float32) / head_size)
    angles = position[:, None] * frequency[None, :]
    return (jnp.cos(angles), jnp.sin(angles))


def rotate(values, cosine_table, sine_table):
    half_size = values.shape[-1] // 2
    first_half = values[..., :half_size]
    second_half = values[..., half_size:]
    cos_wide = cosine_table[:, None, :]
    sin_wide = sine_table[:, None, :]
    return jnp.concatenate(
        [
            first_half * cos_wide - second_half * sin_wide,
            second_half * cos_wide + first_half * sin_wide,
        ],
        axis=-1,
    )


def rotate_back(values, cosine_table, sine_table):
    half_size = values.shape[-1] // 2
    first_half = values[..., :half_size]
    second_half = values[..., half_size:]
    cos_wide = cosine_table[:, None, :]
    sin_wide = sine_table[:, None, :]
    return jnp.concatenate(
        [
            first_half * cos_wide + second_half * sin_wide,
            second_half * cos_wide - first_half * sin_wide,
        ],
        axis=-1,
    )


def normalize(values, gain_vector):
    inverse_rms = lax.rsqrt(jnp.mean(values * values, axis=-1, keepdims=True) + EPS)
    return (values * inverse_rms * gain_vector, inverse_rms)


def normalize_back(values, inverse_rms, gain_vector, upstream):
    weighted = gain_vector * upstream
    return inverse_rms * weighted - values * inverse_rms**3 * jnp.mean(
        values * weighted, axis=-1, keepdims=True
    )


VMEM_SPEC = pl.BlockSpec(memory_space=pltpu.VMEM)
SMEM_SPEC = pl.BlockSpec(memory_space=pltpu.SMEM)
PARAMS = pltpu.CompilerParams(vmem_limit_bytes=60 * 1024 * 1024)


def project_kernel(place, *refs):
    pieces, weights, out = refs[:8], refs[8], refs[9]
    y, zh, c = place[0], place[3], place[4]
    total = None
    for i in range(8):
        block = lax.rem(zh + i // 2, 4)
        core = c if i % 2 == 0 else 1 - c
        part = jnp.dot(
            pieces[i][...],
            weights[lax.rem(block - y + 4, 4), pl.ds(pl.multiple_of(core * 640, 128), 640), :],
            preferred_element_type=F32,
        )
        total = part if total is None else total + part
    out[...] = total


def project(place, pieces, weights):
    return pl.pallas_call(
        project_kernel,
        out_shape=jax.ShapeDtypeStruct((512, 256), F32),
        in_specs=[SMEM_SPEC] + [VMEM_SPEC] * 9,
        out_specs=VMEM_SPEC,
        compiler_params=PARAMS,
        name="project",
    )(place, *pieces, weights)


def weight_grad_kernel(place, *refs):
    pieces, grads, out = refs[:8], refs[8], refs[9]
    zh, c = place[3], place[4]
    for i in range(8):
        feature = 2 * lax.rem(zh + i // 2, 4) + (c if i % 2 == 0 else 1 - c)
        part = lax.dot_general(pieces[i][...], grads[...], TN, preferred_element_type=F32)
        part = part.astype(BF16).reshape(4, 160, 256)
        for j in range(4):
            out[4 * feature + j, 0:160, :] = part[j]


def weight_grad(place, pieces, grads):
    return pl.pallas_call(
        weight_grad_kernel,
        out_shape=jax.ShapeDtypeStruct((32, 160, 256), BF16),
        in_specs=[SMEM_SPEC] + [VMEM_SPEC] * 9,
        out_specs=VMEM_SPEC,
        compiler_params=PARAMS,
        name="weight_grad",
    )(place, *pieces, grads)


def token_grad_kernel(place, own, partner, weights, out):
    y, x, zh, c = place[0], place[1], place[3], place[4]
    total = None
    for i in range(8):
        block = lax.rem(zh + i // 2, 4)
        core = c if i % 2 == 0 else 1 - c
        slot = lax.rem(block - y + 4, 4)
        rows = jnp.concatenate(
            [
                weights[lax.rem(x - core + 4, 4), slot],
                weights[lax.rem(x - core + 2, 4), slot],
            ],
            axis=0,
        )
        source = own if i % 2 == 0 else partner
        part = lax.dot_general(source[i // 2], rows, NT, preferred_element_type=F32)
        total = part if total is None else total + part
    out[...] = total.astype(BF16)


def token_grad_of(place, own, partner, weights):
    return pl.pallas_call(
        token_grad_kernel,
        out_shape=jax.ShapeDtypeStruct((512, 640), BF16),
        in_specs=[SMEM_SPEC] + [VMEM_SPEC] * 3,
        out_specs=VMEM_SPEC,
        compiler_params=PARAMS,
        name="token_grad",
    )(place, own, partner, weights)


def attention(projected, queries, query_gain, key_gain, segments, context_grad):
    head_size = query_gain.shape[0]
    kv_width = head_size
    kv_local = 1
    q_local = queries.shape[1] // head_size
    group_size = q_local // kv_local
    seq_len = queries.shape[0]
    score_scale = head_size ** (-0.5)
    cosine_table, sine_table = rope_tables(segments, head_size)
    key_raw = projected[:, :kv_width].reshape(seq_len, kv_local, head_size)
    value_bf = projected[:, kv_width:].astype(jnp.bfloat16).reshape(seq_len, kv_local, head_size)
    key_normed, key_scale = normalize(key_raw, key_gain)
    key_rot = rotate(key_normed, cosine_table, sine_table).astype(jnp.bfloat16)
    query_wide = queries.astype(jnp.float32).reshape(seq_len, q_local, head_size)
    query_normed, query_scale = normalize(query_wide, query_gain)
    query_rot = (
        rotate(query_normed, cosine_table, sine_table)
        .astype(jnp.bfloat16)
        .reshape(seq_len, kv_local, group_size, head_size)
    )
    grad_rows = context_grad.reshape(seq_len, kv_local, group_size, head_size)
    token_index = jnp.arange(seq_len, dtype=jnp.int32)
    allowed = (segments[:, None] == segments[None, :]) & (
        token_index[None, :] <= token_index[:, None]
    )
    scores = (
        jnp.einsum("qcgh,kch->cgqk", query_rot, key_rot, preferred_element_type=jnp.float32)
        * score_scale
    )
    exponent = jnp.where(allowed, jnp.exp(scores), 0.0)
    weights = exponent / jnp.sum(exponent, axis=-1, keepdims=True)
    rounded = weights.astype(jnp.bfloat16)
    contexts = jnp.einsum(
        "cgqk,kch->qcgh", rounded, value_bf, preferred_element_type=jnp.float32
    ).astype(jnp.bfloat16)
    dot_grad = jnp.einsum("qcgh,kch->cgqk", grad_rows, value_bf, preferred_element_type=jnp.float32)
    delta_row = jnp.sum(weights * dot_grad, axis=-1, keepdims=True)
    score_grad = (weights * (dot_grad - delta_row) * score_scale).astype(jnp.bfloat16)
    value_acc = jnp.einsum("cgqk,qcgh->kch", rounded, grad_rows, preferred_element_type=jnp.float32)
    key_acc = jnp.einsum("cgqk,qcgh->kch", score_grad, query_rot, preferred_element_type=jnp.float32)
    query_grads = jnp.einsum(
        "cgqk,kch->qcgh", score_grad, key_rot, preferred_element_type=jnp.float32
    )
    context = contexts.reshape(seq_len, q_local * head_size)
    query_rot_grad = query_grads.reshape(seq_len, q_local, head_size)
    value_grad = value_acc.astype(jnp.bfloat16).reshape(seq_len, kv_width)
    query_normed_grad = rotate_back(query_rot_grad, cosine_table, sine_table)
    key_normed_grad = rotate_back(key_acc, cosine_table, sine_table)
    query_grad = (
        normalize_back(query_wide, query_scale, query_gain, query_normed_grad)
        .astype(jnp.bfloat16)
        .reshape(seq_len, q_local * head_size)
    )
    key_grad = (
        normalize_back(key_raw, key_scale, key_gain, key_normed_grad)
        .astype(jnp.bfloat16)
        .reshape(seq_len, kv_width)
    )
    gain_query = jnp.sum(query_normed_grad * query_wide * query_scale, axis=(0, 1))
    gain_key = jnp.sum(key_normed_grad * key_raw * key_scale, axis=(0, 1))
    grads = jnp.concatenate([key_grad, value_grad], axis=1)
    return context, query_grad, grads, jnp.concatenate([gain_query, gain_key])[None, :]


def split_pieces(value):
    rows, rest = [], value
    for _ in range(3):
        piece = lax.reduce_precision(rest, 8, 7)
        rows.append(piece)
        rest = rest - piece
    return jnp.concatenate(rows + [jnp.zeros((5, value.shape[1]), F32)], axis=0).astype(BF16)


def ordered_pair(own, other, first):
    return jnp.concatenate([jnp.where(first, own, other), jnp.where(first, other, own)], axis=0)


def local(
    tokens, queries, key_weight, value_weight, query_gain, key_gain, segment_ids, context_grad
):
    node, lane = lax.axis_index("node"), lax.axis_index("local")
    y, x, zl, zh, c = node // 8, node // 2 % 4, node % 2, lane // 2, lane % 2
    place = jnp.stack([y, x, zl, zh, c]).astype(jnp.int32)

    before = shift(tokens, dzh=1)
    after = shift(tokens, dzh=-1)
    stacked = jnp.concatenate([key_weight, value_weight], axis=1)
    columns = ordered_pair(stacked, shift(stacked, dzl=1), zl == 0)
    columns = jnp.roll(jnp.stack(ring(columns, "dx")), x, axis=0).reshape(1280, 256)
    columns = jnp.stack(ring(columns, "dy"))
    rows = send(stacked, lambda y, x, zl, zh, c: (zh, x, zl, y, c))
    rows = ordered_pair(rows, shift(rows, dzl=1), zl == 0)
    rows = jnp.stack(ring(rows, "dy"))
    rows = jnp.stack(
        [
            send(rows, lambda y, x, zl, zh, c, j=j: (y, 2 * (x % 2) + c + j, zl, zh, x // 2))
            for j in range(4)
        ]
    )
    opposite = jnp.concatenate([shift(before[:256], dzh=1), shift(after[256:], dzh=-1)], axis=0)
    pieces = []
    for piece in (tokens, after, opposite, before):
        pieces += [piece, shift(piece, dc=1)]

    projected = project(place, pieces, columns)
    context, query_grad, grads, gains = attention(
        projected, queries, query_gain, key_gain, segment_ids[0], context_grad
    )

    gathered = jnp.stack(ring(grads, "dzh"))
    partial = weight_grad(place, pieces, grads)
    partial = jnp.concatenate(
        [partial, jnp.broadcast_to(split_pieces(gains)[None], (32, 8, 256))], axis=1
    )
    exchanged = lax.all_to_all(partial, "node", 0, 0)
    summed = jnp.sum(exchanged.astype(F32), axis=0)
    weight_sum = summed[:160]
    gains = jnp.sum(summed[160:], axis=0, keepdims=True)
    gains = sum(ring(gains, "dzh"))
    gains = gains + shift(gains, dc=1)
    partner = shift(gathered, dc=1)
    token_grad = token_grad_of(place, gathered, partner, rows)
    return (
        context,
        token_grad,
        query_grad,
        weight_sum[:, :128],
        weight_sum[:, 128:],
        gains.reshape(2, 128),
    )


def solution(mesh):
    in_specs = (
        P("node", "local"),
        P("node", "local"),
        P("node", "local"),
        P("node", "local"),
        P(),
        P(),
        P("node", None),
        P("node", "local"),
    )
    out_specs = (
        P("node", "local"),
        P("node", "local"),
        P("node", "local"),
        P("node", "local"),
        P("node", "local"),
        P(),
    )
    return jax.shard_map(local, mesh=mesh, in_specs=in_specs, out_specs=out_specs, check_vma=False)
```

```python
import jax
import jax.numpy as jnp
from jax import lax
from jax.experimental import pallas as pl
from jax.experimental.pallas import tpu as pltpu
from jax.sharding import PartitionSpec as P

EPS = 1e-06
THETA = 1000000.0
AXES = ("node", "local")
F32 = jnp.float32
BF16 = jnp.bfloat16
NT = (((1,), (1,)), ((), ()))
TN = (((0,), (0,)), ((), ()))
LOG2E = 1.4426950408889634
HEADS = 2
SPANS = ((0, 128), (0, 256), (0, 384), (128, 384))

GROUPS = [[(y * 4 + x) * 2 + zl for y in range(4) for x in range(4)] for zl in range(2)]


def device(y, x, zl, zh, c):
    return (((y % 4) * 4 + x % 4) * 2 + zl % 2) * 8 + (zh % 4) * 2 + c % 2


def send(value, target):
    pairs = [
        (device(y, x, zl, zh, c), device(*target(y, x, zl, zh, c)))
        for y in range(4)
        for x in range(4)
        for zl in range(2)
        for zh in range(4)
        for c in range(2)
    ]
    return lax.ppermute(value, AXES, pairs)


def shift(value, dy=0, dx=0, dzl=0, dzh=0, dc=0):
    return send(value, lambda y, x, zl, zh, c: (y + dy, x + dx, zl + dzl, zh + dzh, c + dc))


def swap(value):
    return lax.all_to_all(value, "node", 0, 0, axis_index_groups=GROUPS)


def gather(value):
    return swap(jnp.broadcast_to(value[None], (16, *value.shape)))


VMEM_SPEC = pl.BlockSpec(memory_space=pltpu.VMEM)
SMEM_SPEC = pl.BlockSpec(memory_space=pltpu.SMEM)
HBM_SPEC = pl.BlockSpec(memory_space=pltpu.HBM)
PARAMS = pltpu.CompilerParams(vmem_limit_bytes=60 * 1024 * 1024)
DMA = pltpu.SemaphoreType.DMA


def on_chip(value):
    return pltpu.with_memory_space_constraint(value, pltpu.VMEM)


def shaped(shape, dtype=BF16):
    return jax.ShapeDtypeStruct(shape, dtype)


def load_pieces(refs, buffer, sems):
    for slot, piece in enumerate(refs):
        step = 512 // len(piece)
        for part, ref in enumerate(piece):
            pltpu.make_async_copy(
                ref, buffer.at[slot, pl.ds(part * step, step)], sems.at[slot]
            ).start()


def wait_piece(buffer, sems, slot):
    pltpu.make_async_copy(buffer.at[slot], buffer.at[slot], sems.at[slot]).wait()


def prep_kernel(segments, frequency, allowed, cosine, sine):
    lane = lax.broadcasted_iota(jnp.int32, (128, 128), 1)
    diagonal = lax.broadcasted_iota(jnp.int32, (128, 128), 0) == lane
    for i in range(4):
        first, width = SPANS[i]
        here = pl.ds(128 * i, 128)
        own = jnp.broadcast_to(segments[:, here].astype(F32), (128, 128))
        own = jnp.sum(jnp.where(diagonal, own, 0.0), axis=1, keepdims=True)
        rows = lax.broadcasted_iota(jnp.int32, (128, width), 0) + 128 * i
        columns = lax.broadcasted_iota(jnp.int32, (128, width), 1) + first
        same = own == segments[:, pl.ds(first, width)].astype(F32)
        mask = jnp.where(same & (columns <= rows), 1.0, 0.0)
        allowed[here, 0:width] = mask
        if width < 384:
            allowed[here, width:384] = jnp.zeros((128, 384 - width), F32)
        position = jnp.sum(mask, axis=1, keepdims=True) - 1.0
        angles = position * frequency[...]
        cosine[here, :] = jnp.cos(angles)
        turn = jnp.sin(angles)
        sine[here, :] = jnp.where(lane < 64, -turn, turn)


def prep(segments):
    frequency = THETA ** (-2.0 * jnp.arange(64, dtype=F32) / 128)
    frequency = jnp.concatenate([frequency, frequency])[None, :]
    return pl.pallas_call(
        prep_kernel,
        out_shape=(shaped((512, 384), F32), shaped((512, 128), F32), shaped((512, 128), F32)),
        in_specs=[VMEM_SPEC, VMEM_SPEC],
        out_specs=(VMEM_SPEC, VMEM_SPEC, VMEM_SPEC),
        compiler_params=PARAMS,
        name="prep",
    )(segments, frequency)


def project_kernel(place, *refs):
    own, partner, halves, wide = refs[0], refs[1], refs[2:10], refs[10]
    out, blocks = refs[11], refs[12:16]
    tokens, sems, block_sems = refs[16:]
    zh, c = place[3], place[4]
    pieces = [(own,), (partner,)] + [halves[2 * k : 2 * k + 2] for k in range(4)]
    load_pieces(pieces, tokens, sems)
    stores = [
        pltpu.make_async_copy(wide.at[lax.rem(zh + r, 4)], blocks[r], block_sems.at[r])
        for r in range(4)
    ]
    for store in stores:
        store.start()
    total = None
    for slot in range(6):
        block = lax.rem(zh + (0, 0, 1, 1, 3, 3)[slot], 4)
        core = c if slot % 2 == 0 else 1 - c
        wait_piece(tokens, sems, slot)
        part = jnp.dot(
            tokens[slot],
            wide[block, pl.ds(pl.multiple_of(core * 640, 128), 640), :],
            preferred_element_type=F32,
        )
        total = part if total is None else total + part
    out[...] = total
    for store in stores:
        store.wait()


def project(place, full, halves, weights):
    return pl.pallas_call(
        project_kernel,
        out_shape=(shaped((512, 256), F32),) + (shaped((1280, 256)),) * 4,
        in_specs=[SMEM_SPEC] + [HBM_SPEC] * 10 + [VMEM_SPEC],
        out_specs=(VMEM_SPEC,) + (HBM_SPEC,) * 4,
        scratch_shapes=[
            pltpu.VMEM((6, 512, 640), BF16),
            DMA((6,)),
            DMA((4,)),
        ],
        compiler_params=PARAMS,
        name="project",
    )(place, *full, *halves, on_chip(weights))


def weight_grad_kernel(place, *refs):
    own, partner, halves, grads = refs[0], refs[1], refs[2:14], refs[14]
    out, tokens, partial, sems, out_sems = refs[15:]
    zh, c = place[3], place[4]
    pieces = [(own,), (partner,)] + [halves[2 * k : 2 * k + 2] for k in range(6)]
    load_pieces(pieces, tokens, sems)

    def store(slot):
        turn = jnp.where(slot < 4, slot // 2, 5 - slot // 2)
        core = jnp.where(slot % 2 == 0, c, 1 - c)
        start = pl.multiple_of((2 * lax.rem(zh + turn, 4) + core) * 640, 128)
        return pltpu.make_async_copy(
            partial.at[slot], out.at[pl.ds(start, 640)], out_sems.at[slot]
        )

    def step(slot, carry):
        wait_piece(tokens, sems, slot)
        part = lax.dot_general(
            tokens[slot], grads[...], TN, preferred_element_type=F32
        )
        partial[slot] = part.astype(BF16)
        store(slot).start()
        return carry

    lax.fori_loop(0, 8, step, 0)
    for slot in range(8):
        store(slot).wait()


def weight_grad(place, full, halves, grads):
    return pl.pallas_call(
        weight_grad_kernel,
        out_shape=shaped((5120, 256)),
        in_specs=[SMEM_SPEC] + [HBM_SPEC] * 14 + [VMEM_SPEC],
        out_specs=HBM_SPEC,
        scratch_shapes=[
            pltpu.VMEM((8, 512, 640), BF16),
            pltpu.VMEM((8, 640, 256), BF16),
            DMA((8,)),
            DMA((8,)),
        ],
        compiler_params=PARAMS,
        name="weight_grad",
    )(place, *full, *halves, grads)


def sum_rows_kernel(place, parts, keep, away):
    zl = place[2]
    for out, half in ((keep, zl), (away, 1 - zl)):
        rows = pl.ds(pl.multiple_of(half * 160, 32), 160)
        total = parts[0, rows].astype(F32)
        for r in range(1, 16):
            total = total + parts[r, rows].astype(F32)
        out[...] = total


def sum_rows(place, parts):
    return pl.pallas_call(
        sum_rows_kernel,
        out_shape=(shaped((160, 256), F32), shaped((160, 256), F32)),
        in_specs=[SMEM_SPEC, VMEM_SPEC],
        out_specs=(VMEM_SPEC, VMEM_SPEC),
        compiler_params=PARAMS,
        name="sum_rows",
    )(place, on_chip(parts))


def sum_last_kernel(keep, away, key_out, value_out):
    total = keep[...] + away[...]
    key_out[...] = total[:, :128]
    value_out[...] = total[:, 128:]


def small(kernel, outs, *operands):
    specs = [SMEM_SPEC if o.ndim == 1 else VMEM_SPEC for o in operands]
    return pl.pallas_call(
        kernel,
        out_shape=tuple(outs),
        in_specs=specs,
        out_specs=tuple([VMEM_SPEC] * len(outs)),
        compiler_params=PARAMS,
    )(*(o if o.ndim == 1 else on_chip(o) for o in operands))


def token_grad_kernel(place, *refs):
    count = len(refs) // 2 - 1
    grads, weights, (mine, theirs) = refs[:count], refs[count : 2 * count], refs[2 * count :]
    c = place[4]
    for out, core in ((theirs, 1 - c), (mine, c)):
        rows = pl.ds(pl.multiple_of(core * 640, 128), 640)
        total = None
        for grad, weight in zip(grads, weights):
            part = lax.dot_general(grad[...], weight[rows, :], NT, preferred_element_type=F32)
            total = part if total is None else total + part
        out[...] = total.astype(out.dtype)


def token_grad_of(place, grads, weights):
    return small(
        token_grad_kernel,
        [shaped((512, 640), F32), shaped((512, 640))],
        place, *grads, *weights,
    )


def attention_kernel(
    place, partial, top, bottom, top_partner, bottom_partner, opposite, queries, grads_in, cosine, sine, allowed, query_gain, key_gain,
    context, query_grad, grads, gains_out, cross_mine, cross_theirs,
    raw, key_rot, value, key_acc, value_acc, gains,
):
    step = pl.program_id(0)
    scale = 128**-0.5

    @pl.when(step == 0)
    def _():
        core = place[4]
        mine = opposite[pl.ds(pl.multiple_of(core * 640, 128), 640), :]
        other = opposite[pl.ds(pl.multiple_of((1 - core) * 640, 128), 640), :]
        for half, (a, b) in enumerate(((top, top_partner), (bottom, bottom_partner))):
            rows = pl.ds(256 * half, 256)
            raw[rows, :] = (
                partial[rows, :]
                + jnp.dot(a[...], mine, preferred_element_type=F32)
                + jnp.dot(b[...], other, preferred_element_type=F32)
            )
        key_raw = raw[:, :128]
        inverse = lax.rsqrt(jnp.mean(key_raw * key_raw, axis=-1, keepdims=True) + EPS)
        normed = key_raw * inverse * key_gain[...]
        key_rot[...] = (normed * cosine[...] + pltpu.roll(normed, 64, 1) * sine[...]).astype(BF16)
        value[...] = raw[:, 128:].astype(BF16)
        key_acc[...] = jnp.zeros_like(key_acc)
        value_acc[...] = jnp.zeros_like(value_acc)
        gains[...] = jnp.zeros_like(gains)

    gain = query_gain[...]
    gain_sum = jnp.zeros((1, 128), F32)

    def heads(ref, rows):
        return jnp.concatenate([ref[rows, pl.ds(128 * h, 128)] for h in range(HEADS)], axis=0)

    def again(tile):
        return jnp.concatenate([tile] * HEADS, axis=0)

    for i in range(4):
        first, width = SPANS[i]
        here, span = pl.ds(128 * i, 128), pl.ds(first, width)
        query = heads(queries, here).astype(F32)
        inverse = lax.rsqrt(jnp.mean(query * query, axis=-1, keepdims=True) + EPS)
        scaled = query * inverse
        normed = scaled * gain
        cos, sin = again(cosine[here, :]), again(sine[here, :])
        query_rot = (normed * cos + pltpu.roll(normed, 64, 1) * sin).astype(BF16)
        keys, values, upstream = key_rot[span, :], value[span, :], heads(grads_in, here)
        scores = lax.dot_general(query_rot, keys, NT, preferred_element_type=F32)
        exponent = jnp.exp2(scores * (scale * LOG2E)) * again(allowed[here, pl.ds(0, width)])
        weights = exponent * (1.0 / jnp.sum(exponent, axis=-1, keepdims=True))
        rounded = weights.astype(BF16)
        mixed = jnp.dot(rounded, values, preferred_element_type=F32).astype(BF16)
        dot_grad = lax.dot_general(upstream, values, NT, preferred_element_type=F32)
        delta = jnp.sum(weights * dot_grad, axis=-1, keepdims=True)
        score_grad = (weights * (dot_grad - delta)).astype(BF16)
        value_acc[span, :] += lax.dot_general(rounded, upstream, TN, preferred_element_type=F32)
        key_acc[span, :] += lax.dot_general(score_grad, query_rot, TN, preferred_element_type=F32)
        rot_grad = jnp.dot(score_grad, keys, preferred_element_type=F32) * scale
        normed_grad = rot_grad * cos - pltpu.roll(rot_grad, 64, 1) * sin
        gain_sum += jnp.sum(normed_grad * scaled, axis=0, keepdims=True)
        weighted = gain * normed_grad
        mean = jnp.mean(scaled * weighted, axis=-1, keepdims=True)
        raw_grad = (inverse * (weighted - scaled * mean)).astype(BF16)
        for h in range(HEADS):
            context[here, pl.ds(128 * h, 128)] = mixed[128 * h : 128 * h + 128]
            query_grad[here, pl.ds(128 * h, 128)] = raw_grad[128 * h : 128 * h + 128]
    gains[0:1, :] += gain_sum

    @pl.when(step == pl.num_programs(0) - 1)
    def _():
        key_raw = raw[:, :128]
        inverse = lax.rsqrt(jnp.mean(key_raw * key_raw, axis=-1, keepdims=True) + EPS)
        scaled = key_raw * inverse
        rot_grad = key_acc[...] * scale
        normed_grad = rot_grad * cosine[...] - pltpu.roll(rot_grad, 64, 1) * sine[...]
        gains[1:2, :] = jnp.sum(normed_grad * scaled, axis=0, keepdims=True)
        weighted = key_gain[...] * normed_grad
        mean = jnp.mean(scaled * weighted, axis=-1, keepdims=True)
        grads[:, :128] = (inverse * (weighted - scaled * mean)).astype(BF16)
        grads[:, 128:] = value_acc[...].astype(BF16)
        for r in range(16):
            gains_out[r] = gains[...]
        core = place[4]
        for out, half in ((cross_theirs, 1 - core), (cross_mine, core)):
            rows = pl.ds(pl.multiple_of(half * 640, 128), 640)
            part = lax.dot_general(
                grads[...], opposite[rows, :], NT, preferred_element_type=F32
            )
            out[...] = part.astype(out.dtype)


def attention(place, partial, last, opposite, queries, query_gain, key_gain, tables, context_grad):
    allowed, cosine, sine = tables
    head = pl.BlockSpec((512, 128 * HEADS), lambda h: (0, h))

    def whole(*shape):
        return pl.BlockSpec(shape, lambda h: (0, 0))

    return pl.pallas_call(
        attention_kernel,
        grid=(8 // HEADS,),
        out_shape=(
            jax.ShapeDtypeStruct((512, 1024), BF16),
            jax.ShapeDtypeStruct((512, 1024), BF16),
            jax.ShapeDtypeStruct((512, 256), BF16),
            jax.ShapeDtypeStruct((16, 8, 128), F32),
            jax.ShapeDtypeStruct((512, 640), F32),
            jax.ShapeDtypeStruct((512, 640), BF16),
        ),
        in_specs=[
            SMEM_SPEC, whole(512, 256), *[VMEM_SPEC] * 4, whole(1280, 256), head, head, whole(512, 128), whole(512, 128),
            whole(512, 384), whole(1, 128), whole(1, 128),
        ],
        out_specs=(
            head, head, whole(512, 256), pl.BlockSpec((16, 8, 128), lambda h: (0, 0, 0)),
            whole(512, 640), whole(512, 640),
        ),
        scratch_shapes=[
            pltpu.VMEM((512, 256), F32),
            pltpu.VMEM((512, 128), BF16),
            pltpu.VMEM((512, 128), BF16),
            pltpu.VMEM((512, 128), F32),
            pltpu.VMEM((512, 128), F32),
            pltpu.VMEM((8, 128), F32),
        ],
        compiler_params=pltpu.CompilerParams(
            vmem_limit_bytes=60 * 1024 * 1024, dimension_semantics=("arbitrary",)
        ),
        name="attention",
    )(
        place, partial, *map(on_chip, last), opposite, queries, context_grad, cosine, sine,
        allowed, query_gain[None, :], key_gain[None, :],
    )


def pair_of(value, zl):
    other = shift(value, dzl=1)
    first = zl == 0
    return jnp.concatenate(
        [jnp.where(first, value, other), jnp.where(first, other, value)], axis=0
    )


def local(
    tokens, queries, key_weight, value_weight, query_gain, key_gain, segment_ids, context_grad
):
    node, lane = lax.axis_index("node"), lax.axis_index("local")
    y, x, zl, zh, c = node // 8, node // 2 % 4, node % 2, lane // 2, lane % 2
    place = jnp.stack([y, x, zl, zh, c]).astype(jnp.int32)

    pair = jnp.concatenate([pair_of(key_weight, zl), pair_of(value_weight, zl)], axis=1)
    columns = gather(pair).reshape(4, 1280, 256)
    top, bottom = tokens[:256], tokens[256:]
    before = [shift(top, dzh=1), shift(bottom, dzh=1)]
    after = [shift(top, dzh=-1), shift(bottom, dzh=-1)]
    opposite = [shift(before[0], dzh=1), shift(after[1], dzh=-1)]
    full = [tokens, shift(tokens, dc=1)]
    before += [shift(before[0], dc=1), shift(before[1], dc=1)]
    after += [shift(after[0], dc=1), shift(after[1], dc=1)]
    opposite += [shift(opposite[0], dc=1), shift(opposite[1], dc=1)]
    tables = prep(segment_ids)
    partial, *blocks = project(place, full, after + before, columns)
    rows_after = shift(blocks[3], dzh=-1)
    rows_before = shift(blocks[1], dzh=1)
    context, query_grad, grads, gains, mine, theirs = attention(
        place, partial, opposite, blocks[2], queries, query_gain, key_gain, tables,
        context_grad,
    )

    weight_part = weight_grad(place, full, after + before + opposite, grads)
    gains = jnp.sum(swap(gains), axis=0)
    weight_part = swap(weight_part.reshape(16, 320, 256))
    grads_after = shift(grads, dzh=-1)
    grads_before = shift(grads, dzh=1)
    crossed = (mine + shift(theirs, dc=1).astype(F32)).astype(BF16)
    crossed = shift(crossed, dzh=2)
    gains += send(gains, lambda y, x, zl, zh, c: (y, x, zl, zh ^ 1, c))
    gains += send(gains, lambda y, x, zl, zh, c: (y, x, zl, zh ^ 2, c))
    mine, theirs = token_grad_of(
        place, [grads, grads_after, grads_before], [blocks[0], rows_after, rows_before]
    )
    token_grad = mine + shift(theirs, dc=1).astype(F32) + crossed.astype(F32)
    gains = gains + shift(gains, dzl=1)
    gains = gains + shift(gains, dc=1)
    keep, away = sum_rows(place, weight_part)
    key_weight_grad, value_weight_grad = small(
        sum_last_kernel,
        [shaped((160, 128), F32)] * 2,
        keep, shift(away, dzl=1),
    )
    return (
        context,
        token_grad.astype(BF16),
        query_grad,
        key_weight_grad,
        value_weight_grad,
        gains[:2],
    )


def solution(mesh):
    in_specs = (
        P("node", "local"),
        P("node", "local"),
        P("node", "local"),
        P("node", "local"),
        P(),
        P(),
        P("node", None),
        P("node", "local"),
    )
    out_specs = (
        P("node", "local"),
        P("node", "local"),
        P("node", "local"),
        P("node", "local"),
        P("node", "local"),
        P(),
    )
    return jax.shard_map(local, mesh=mesh, in_specs=in_specs, out_specs=out_specs, check_vma=False)
```

```python
import jax
import jax.numpy as jnp
from jax import lax
from jax.experimental import pallas as pl
from jax.experimental.pallas import tpu as pltpu
from jax.sharding import PartitionSpec as P

EPS = 1e-06
THETA = 1000000.0
AXES = ("node", "local")
F32 = jnp.float32
BF16 = jnp.bfloat16
NT = (((1,), (1,)), ((), ()))
TN = (((0,), (0,)), ((), ()))
LOG2E = 1.4426950408889634
HEADS = 4
SPANS = ((0, 128), (0, 256), (0, 384), (128, 384))

GROUPS = [[(y * 4 + x) * 2 + zl for y in range(4) for x in range(4)] for zl in range(2)]


def device(y, x, zl, zh, c):
    return (((y % 4) * 4 + x % 4) * 2 + zl % 2) * 8 + (zh % 4) * 2 + c % 2


def send(value, target):
    pairs = [
        (device(y, x, zl, zh, c), device(*target(y, x, zl, zh, c)))
        for y in range(4)
        for x in range(4)
        for zl in range(2)
        for zh in range(4)
        for c in range(2)
    ]
    return lax.ppermute(value, AXES, pairs)


def shift(value, dy=0, dx=0, dzl=0, dzh=0, dc=0):
    return send(value, lambda y, x, zl, zh, c: (y + dy, x + dx, zl + dzl, zh + dzh, c + dc))


def swap(value):
    return lax.all_to_all(value, "node", 0, 0, axis_index_groups=GROUPS)


def gather(value):
    return swap(jnp.broadcast_to(value[None], (16, *value.shape)))


VMEM_SPEC = pl.BlockSpec(memory_space=pltpu.VMEM)
SMEM_SPEC = pl.BlockSpec(memory_space=pltpu.SMEM)
HBM_SPEC = pl.BlockSpec(memory_space=pltpu.HBM)
PARAMS = pltpu.CompilerParams(vmem_limit_bytes=60 * 1024 * 1024)
DMA = pltpu.SemaphoreType.DMA


def on_chip(value):
    return pltpu.with_memory_space_constraint(value, pltpu.VMEM)


def shaped(shape, dtype=BF16):
    return jax.ShapeDtypeStruct(shape, dtype)


def load_pieces(refs, buffer, sems):
    for slot, piece in enumerate(refs):
        step = 512 // len(piece)
        for part, ref in enumerate(piece):
            pltpu.make_async_copy(
                ref, buffer.at[slot, pl.ds(part * step, step)], sems.at[slot]
            ).start()


def wait_piece(buffer, sems, slot):
    pltpu.make_async_copy(buffer.at[slot], buffer.at[slot], sems.at[slot]).wait()


def prep_kernel(
    segments, frequency, queries, query_gain, allowed, cosine, sine, rotated, scaled, inverses
):
    lane = lax.broadcasted_iota(jnp.int32, (128, 128), 1)
    diagonal = lax.broadcasted_iota(jnp.int32, (128, 128), 0) == lane
    for i in range(4):
        first, width = SPANS[i]
        here = pl.ds(128 * i, 128)
        own = jnp.broadcast_to(segments[:, here].astype(F32), (128, 128))
        own = jnp.sum(jnp.where(diagonal, own, 0.0), axis=1, keepdims=True)
        rows = lax.broadcasted_iota(jnp.int32, (128, width), 0) + 128 * i
        columns = lax.broadcasted_iota(jnp.int32, (128, width), 1) + first
        same = own == segments[:, pl.ds(first, width)].astype(F32)
        mask = jnp.where(same & (columns <= rows), 1.0, 0.0)
        allowed[here, 0:width] = mask
        if width < 384:
            allowed[here, width:384] = jnp.zeros((128, 384 - width), F32)
        position = jnp.sum(mask, axis=1, keepdims=True) - 1.0
        angles = position * frequency[...]
        cosine[here, :] = jnp.cos(angles)
        turn = jnp.sin(angles)
        sine[here, :] = jnp.where(lane < 64, -turn, turn)

    def head(h, carry):
        columns = pl.ds(pl.multiple_of(128 * h, 128), 128)
        for i in range(4):
            here = pl.ds(128 * i, 128)
            query = queries[here, columns].astype(F32)
            inverse = lax.rsqrt(jnp.mean(query * query, axis=-1, keepdims=True) + EPS)
            unit = query * inverse
            normed = unit * query_gain[...]
            turned = normed * cosine[here, :] + pltpu.roll(normed, 64, 1) * sine[here, :]
            rotated[here, columns] = turned.astype(BF16)
            scaled[here, columns] = unit
            inverses[here, columns] = jnp.broadcast_to(inverse, (128, 128))
        return carry

    lax.fori_loop(0, 8, head, 0)


def prep(segments, queries, query_gain):
    frequency = THETA ** (-2.0 * jnp.arange(64, dtype=F32) / 128)
    frequency = jnp.concatenate([frequency, frequency])[None, :]
    return pl.pallas_call(
        prep_kernel,
        out_shape=(
            shaped((512, 384), F32), shaped((512, 128), F32), shaped((512, 128), F32),
            shaped((512, 1024)), shaped((512, 1024), F32), shaped((512, 1024), F32),
        ),
        in_specs=[VMEM_SPEC] * 4,
        out_specs=(VMEM_SPEC,) * 6,
        compiler_params=PARAMS,
        name="prep",
    )(segments, frequency, queries, query_gain[None, :])


def project_kernel(place, *refs):
    pieces, wide = refs[:6], refs[6]
    out, blocks = refs[7], refs[8:12]
    tokens, sems, block_sems = refs[12:]
    zh, c = place[3], place[4]
    load_pieces([(piece,) for piece in pieces], tokens, sems)
    stores = [
        pltpu.make_async_copy(wide.at[lax.rem(zh + r, 4)], blocks[r], block_sems.at[r])
        for r in range(4)
    ]
    for store in stores:
        store.start()
    total = None
    for slot in range(6):
        block = lax.rem(zh + (0, 0, 1, 1, 3, 3)[slot], 4)
        core = c if slot % 2 == 0 else 1 - c
        wait_piece(tokens, sems, slot)
        part = jnp.dot(
            tokens[slot],
            wide[block, pl.ds(pl.multiple_of(core * 640, 128), 640), :],
            preferred_element_type=F32,
        )
        total = part if total is None else total + part
    out[...] = total
    for store in stores:
        store.wait()


def project(place, full, weights):
    return pl.pallas_call(
        project_kernel,
        out_shape=(shaped((512, 256), F32),) + (shaped((1280, 256)),) * 4,
        in_specs=[SMEM_SPEC] + [HBM_SPEC] * 6 + [VMEM_SPEC],
        out_specs=(VMEM_SPEC,) + (HBM_SPEC,) * 4,
        scratch_shapes=[
            pltpu.VMEM((6, 512, 640), BF16),
            DMA((6,)),
            DMA((4,)),
        ],
        compiler_params=PARAMS,
        name="project",
    )(place, *full, on_chip(weights))


def weight_grad_kernel(place, *refs):
    pieces, last, grads, mine_hbm, theirs = refs[:6], refs[6:10], *refs[10:13]
    out, crossed, tokens, partial, sems, out_sems = refs[13:19]
    mine, mine_sem = refs[19:]
    zh, c = place[3], place[4]
    load_pieces([(piece,) for piece in pieces] + [last[:2], last[2:]], tokens, sems)
    copy = pltpu.make_async_copy(mine_hbm, mine, mine_sem)
    copy.start()

    def store(slot):
        turn = jnp.where(slot < 4, slot // 2, 5 - slot // 2)
        core = jnp.where(slot % 2 == 0, c, 1 - c)
        start = pl.multiple_of((2 * lax.rem(zh + turn, 4) + core) * 640, 128)
        return pltpu.make_async_copy(
            partial.at[slot], out.at[pl.ds(start, 640)], out_sems.at[slot]
        )

    def step(slot, carry):
        wait_piece(tokens, sems, slot)
        part = lax.dot_general(
            tokens[slot], grads[...], TN, preferred_element_type=F32
        )
        partial[slot] = part.astype(BF16)
        store(slot).start()
        return carry

    lax.fori_loop(0, 8, step, 0)
    copy.wait()
    crossed[...] = (mine[...] + theirs[...].astype(F32)).astype(BF16)
    for slot in range(8):
        store(slot).wait()


def weight_grad(place, full, halves, grads, mine, theirs):
    return pl.pallas_call(
        weight_grad_kernel,
        out_shape=(shaped((5120, 256)), shaped((512, 640))),
        in_specs=[SMEM_SPEC] + [HBM_SPEC] * 10 + [VMEM_SPEC, HBM_SPEC, VMEM_SPEC],
        out_specs=(HBM_SPEC, VMEM_SPEC),
        scratch_shapes=[
            pltpu.VMEM((8, 512, 640), BF16),
            pltpu.VMEM((8, 640, 256), BF16),
            DMA((8,)),
            DMA((8,)),
            pltpu.VMEM((512, 640), F32),
            DMA,
        ],
        compiler_params=PARAMS,
        name="weight_grad",
    )(place, *full, *halves, grads, mine, on_chip(theirs))


def sum_rows_kernel(place, parts, gains, keep, away):
    zl = place[2]
    for out, half in ((keep, zl), (away, 1 - zl)):
        out[160:168, 0:128] = gains[...]
        out[160:168, 128:256] = gains[...]
        rows = pl.ds(pl.multiple_of(half * 160, 32), 160)
        total = parts[0, rows].astype(F32)
        for r in range(1, 16):
            total = total + parts[r, rows].astype(F32)
        out[0:160, :] = total


def sum_rows(place, parts, gains):
    return pl.pallas_call(
        sum_rows_kernel,
        out_shape=(shaped((168, 256), F32), shaped((168, 256), F32)),
        in_specs=[SMEM_SPEC, VMEM_SPEC, VMEM_SPEC],
        out_specs=(VMEM_SPEC, VMEM_SPEC),
        compiler_params=PARAMS,
        name="sum_rows",
    )(place, on_chip(parts), gains)


def sum_last_kernel(keep, away, key_out, value_out, gains):
    total = keep[...] + away[...]
    key_out[...] = total[:160, :128]
    value_out[...] = total[:160, 128:]
    gains[...] = total[160:162, :128]


def small(kernel, outs, *operands):
    specs = [SMEM_SPEC if o.ndim == 1 else VMEM_SPEC for o in operands]
    return pl.pallas_call(
        kernel,
        out_shape=tuple(outs),
        in_specs=specs,
        out_specs=tuple([VMEM_SPEC] * len(outs)),
        compiler_params=PARAMS,
    )(*(o if o.ndim == 1 else on_chip(o) for o in operands))


def token_grad_kernel(place, *refs):
    count = len(refs) // 2 - 1
    grads, weights, (mine, theirs) = refs[:count], refs[count : 2 * count], refs[2 * count :]
    c = place[4]
    for out, core in ((theirs, 1 - c), (mine, c)):
        rows = pl.ds(pl.multiple_of(core * 640, 128), 640)
        total = None
        for grad, weight in zip(grads, weights):
            part = lax.dot_general(grad[...], weight[rows, :], NT, preferred_element_type=F32)
            total = part if total is None else total + part
        out[...] = total.astype(out.dtype)


def token_grad_of(place, grads, weights):
    return small(
        token_grad_kernel,
        [shaped((512, 640), F32), shaped((512, 640))],
        place, *grads, *weights,
    )


def attention_kernel(
    place, partial, top, bottom, top_partner, bottom_partner, opposite, rotated, scaled_in, inverses, grads_in,
    cosine, sine, allowed, query_gain, key_gain,
    context, query_grad, grads, gains_out, cross_mine, cross_theirs,
    raw, key_rot, value, key_acc, value_acc, gains,
):
    step = pl.program_id(0)
    scale = 128**-0.5

    @pl.when(step == 0)
    def _():
        core = place[4]
        mine = opposite[pl.ds(pl.multiple_of(core * 640, 128), 640), :]
        other = opposite[pl.ds(pl.multiple_of((1 - core) * 640, 128), 640), :]
        for half, (a, b) in enumerate(((top, top_partner), (bottom, bottom_partner))):
            rows = pl.ds(256 * half, 256)
            raw[rows, :] = (
                partial[rows, :]
                + jnp.dot(a[...], mine, preferred_element_type=F32)
                + jnp.dot(b[...], other, preferred_element_type=F32)
            )
        key_raw = raw[:, :128]
        inverse = lax.rsqrt(jnp.mean(key_raw * key_raw, axis=-1, keepdims=True) + EPS)
        normed = key_raw * inverse * key_gain[...]
        key_rot[...] = (normed * cosine[...] + pltpu.roll(normed, 64, 1) * sine[...]).astype(BF16)
        value[...] = raw[:, 128:].astype(BF16)
        key_acc[...] = jnp.zeros_like(key_acc)
        value_acc[...] = jnp.zeros_like(value_acc)
        gains[...] = jnp.zeros_like(gains)

    gain = query_gain[...]
    gain_sum = jnp.zeros((1, 128), F32)

    def heads(ref, rows):
        return jnp.concatenate([ref[rows, pl.ds(128 * h, 128)] for h in range(HEADS)], axis=0)

    def again(tile):
        return jnp.concatenate([tile] * HEADS, axis=0)

    for i in range(4):
        first, width = SPANS[i]
        here, span = pl.ds(128 * i, 128), pl.ds(first, width)
        query_rot, scaled = heads(rotated, here), heads(scaled_in, here)
        inverse = heads(inverses, here)
        cos, sin = again(cosine[here, :]), again(sine[here, :])
        keys, values, upstream = key_rot[span, :], value[span, :], heads(grads_in, here)
        scores = lax.dot_general(query_rot, keys, NT, preferred_element_type=F32)
        exponent = jnp.exp2(scores * (scale * LOG2E)) * again(allowed[here, pl.ds(0, width)])
        weights = exponent * (1.0 / jnp.sum(exponent, axis=-1, keepdims=True))
        rounded = weights.astype(BF16)
        mixed = jnp.dot(rounded, values, preferred_element_type=F32).astype(BF16)
        dot_grad = lax.dot_general(upstream, values, NT, preferred_element_type=F32)
        delta = jnp.sum(weights * dot_grad, axis=-1, keepdims=True)
        score_grad = (weights * (dot_grad - delta)).astype(BF16)
        value_acc[span, :] += lax.dot_general(rounded, upstream, TN, preferred_element_type=F32)
        key_acc[span, :] += lax.dot_general(score_grad, query_rot, TN, preferred_element_type=F32)
        rot_grad = jnp.dot(score_grad, keys, preferred_element_type=F32) * scale
        normed_grad = rot_grad * cos - pltpu.roll(rot_grad, 64, 1) * sin
        gain_sum += jnp.sum(normed_grad * scaled, axis=0, keepdims=True)
        weighted = gain * normed_grad
        mean = jnp.mean(scaled * weighted, axis=-1, keepdims=True)
        raw_grad = (inverse * (weighted - scaled * mean)).astype(BF16)
        for h in range(HEADS):
            context[here, pl.ds(128 * h, 128)] = mixed[128 * h : 128 * h + 128]
            query_grad[here, pl.ds(128 * h, 128)] = raw_grad[128 * h : 128 * h + 128]
    gains[0:1, :] += gain_sum

    @pl.when(step == pl.num_programs(0) - 1)
    def _():
        key_raw = raw[:, :128]
        inverse = lax.rsqrt(jnp.mean(key_raw * key_raw, axis=-1, keepdims=True) + EPS)
        scaled = key_raw * inverse
        rot_grad = key_acc[...] * scale
        normed_grad = rot_grad * cosine[...] - pltpu.roll(rot_grad, 64, 1) * sine[...]
        gains[1:2, :] = jnp.sum(normed_grad * scaled, axis=0, keepdims=True)
        weighted = key_gain[...] * normed_grad
        mean = jnp.mean(scaled * weighted, axis=-1, keepdims=True)
        grads[:, :128] = (inverse * (weighted - scaled * mean)).astype(BF16)
        grads[:, 128:] = value_acc[...].astype(BF16)
        for r in range(16):
            gains_out[r] = gains[...]
        core = place[4]
        for out, half in ((cross_theirs, 1 - core), (cross_mine, core)):
            rows = pl.ds(pl.multiple_of(half * 640, 128), 640)
            part = lax.dot_general(
                grads[...], opposite[rows, :], NT, preferred_element_type=F32
            )
            out[...] = part.astype(out.dtype)


def attention(place, partial, last, opposite, query_gain, key_gain, tables, context_grad):
    allowed, cosine, sine, *prepared = tables
    head = pl.BlockSpec((512, 128 * HEADS), lambda h: (0, h))

    def whole(*shape):
        return pl.BlockSpec(shape, lambda h: (0, 0))

    return pl.pallas_call(
        attention_kernel,
        grid=(8 // HEADS,),
        out_shape=(
            jax.ShapeDtypeStruct((512, 1024), BF16),
            jax.ShapeDtypeStruct((512, 1024), BF16),
            jax.ShapeDtypeStruct((512, 256), BF16),
            jax.ShapeDtypeStruct((16, 8, 128), F32),
            jax.ShapeDtypeStruct((512, 640), F32),
            jax.ShapeDtypeStruct((512, 640), BF16),
        ),
        in_specs=[
            SMEM_SPEC, whole(512, 256), *[VMEM_SPEC] * 4, whole(1280, 256), *[head] * 4, whole(512, 128), whole(512, 128),
            whole(512, 384), whole(1, 128), whole(1, 128),
        ],
        out_specs=(
            head, head, whole(512, 256), pl.BlockSpec((16, 8, 128), lambda h: (0, 0, 0)),
            whole(512, 640), whole(512, 640),
        ),
        scratch_shapes=[
            pltpu.VMEM((512, 256), F32),
            pltpu.VMEM((512, 128), BF16),
            pltpu.VMEM((512, 128), BF16),
            pltpu.VMEM((512, 128), F32),
            pltpu.VMEM((512, 128), F32),
            pltpu.VMEM((8, 128), F32),
        ],
        compiler_params=pltpu.CompilerParams(
            vmem_limit_bytes=60 * 1024 * 1024, dimension_semantics=("arbitrary",)
        ),
        name="attention",
    )(
        place, partial, *map(on_chip, last), opposite, *prepared, context_grad, cosine, sine,
        allowed, query_gain[None, :], key_gain[None, :],
    )


def pair_of(value, zl):
    other = shift(value, dzl=1)
    first = zl == 0
    return jnp.concatenate(
        [jnp.where(first, value, other), jnp.where(first, other, value)], axis=0
    )


def local(
    tokens, queries, key_weight, value_weight, query_gain, key_gain, segment_ids, context_grad
):
    node, lane = lax.axis_index("node"), lax.axis_index("local")
    y, x, zl, zh, c = node // 8, node // 2 % 4, node % 2, lane // 2, lane % 2
    place = jnp.stack([y, x, zl, zh, c]).astype(jnp.int32)

    pair = jnp.concatenate([pair_of(key_weight, zl), pair_of(value_weight, zl)], axis=1)
    columns = gather(pair).reshape(4, 1280, 256)
    before, after = shift(tokens, dzh=1), shift(tokens, dzh=-1)
    opposite = [shift(before[:256], dzh=1), shift(after[256:], dzh=-1)]
    full = [tokens, shift(tokens, dc=1), after, shift(after, dc=1)]
    full += [before, shift(before, dc=1)]
    opposite += [shift(opposite[0], dc=1), shift(opposite[1], dc=1)]
    tables = prep(segment_ids, queries, query_gain)
    partial, *blocks = project(place, full, columns)
    rows_after = shift(blocks[3], dzh=-1)
    rows_before = shift(blocks[1], dzh=1)
    context, query_grad, grads, gains, mine, theirs = attention(
        place, partial, opposite, blocks[2], query_gain, key_gain, tables,
        context_grad,
    )

    weight_part, crossed = weight_grad(place, full, opposite, grads, mine, shift(theirs, dc=1))
    gains = jnp.sum(swap(gains), axis=0)
    gains += send(gains, lambda y, x, zl, zh, c: (y, x, zl, zh ^ 1, c))
    gains += send(gains, lambda y, x, zl, zh, c: (y, x, zl, zh ^ 2, c))
    gains += shift(gains, dc=1)
    weight_part = swap(weight_part.reshape(16, 320, 256))
    grads_after = shift(grads, dzh=-1)
    grads_before = shift(grads, dzh=1)
    crossed = shift(crossed, dzh=2)
    mine, theirs = token_grad_of(
        place, [grads, grads_after, grads_before], [blocks[0], rows_after, rows_before]
    )
    token_grad = mine + shift(theirs, dc=1).astype(F32) + crossed.astype(F32)
    keep, away = sum_rows(place, weight_part, gains)
    key_weight_grad, value_weight_grad, gains = small(
        sum_last_kernel,
        [shaped((160, 128), F32)] * 2 + [shaped((2, 128), F32)],
        keep, shift(away, dzl=1),
    )
    return (
        context,
        token_grad.astype(BF16),
        query_grad,
        key_weight_grad,
        value_weight_grad,
        gains,
    )


def solution(mesh):
    in_specs = (
        P("node", "local"),
        P("node", "local"),
        P("node", "local"),
        P("node", "local"),
        P(),
        P(),
        P("node", None),
        P("node", "local"),
    )
    out_specs = (
        P("node", "local"),
        P("node", "local"),
        P("node", "local"),
        P("node", "local"),
        P("node", "local"),
        P(),
    )
    return jax.shard_map(local, mesh=mesh, in_specs=in_specs, out_specs=out_specs, check_vma=False)
```

```python
import jax
import jax.numpy as jnp
from jax import lax
from jax.experimental import pallas as pl
from jax.experimental.pallas import tpu as pltpu
from jax.sharding import PartitionSpec as P

EPS = 1e-06
THETA = 1000000.0
AXES = ("node", "local")
F32 = jnp.float32
BF16 = jnp.bfloat16
NT = (((1,), (1,)), ((), ()))
TN = (((0,), (0,)), ((), ()))
LOG2E = 1.4426950408889634
HEADS = 8
SPANS = ((0, 128), (0, 256), (0, 384), (128, 384))

GROUPS = [[(y * 4 + x) * 2 + zl for y in range(4) for x in range(4)] for zl in range(2)]


def device(y, x, zl, zh, c):
    return (((y % 4) * 4 + x % 4) * 2 + zl % 2) * 8 + (zh % 4) * 2 + c % 2


def send(value, target):
    pairs = [
        (device(y, x, zl, zh, c), device(*target(y, x, zl, zh, c)))
        for y in range(4)
        for x in range(4)
        for zl in range(2)
        for zh in range(4)
        for c in range(2)
    ]
    return lax.ppermute(value, AXES, pairs)


def shift(value, dy=0, dx=0, dzl=0, dzh=0, dc=0):
    return send(value, lambda y, x, zl, zh, c: (y + dy, x + dx, zl + dzl, zh + dzh, c + dc))


def swap(value):
    return lax.all_to_all(value, "node", 0, 0, axis_index_groups=GROUPS)


VMEM_SPEC = pl.BlockSpec(memory_space=pltpu.VMEM)
SMEM_SPEC = pl.BlockSpec(memory_space=pltpu.SMEM)
HBM_SPEC = pl.BlockSpec(memory_space=pltpu.HBM)
PARAMS = pltpu.CompilerParams(vmem_limit_bytes=60 * 1024 * 1024)
DMA = pltpu.SemaphoreType.DMA


def on_chip(value):
    return pltpu.with_memory_space_constraint(value, pltpu.VMEM)


def shaped(shape, dtype=BF16):
    return jax.ShapeDtypeStruct(shape, dtype)


def load_pieces(refs, buffer, sems):
    for slot, piece in enumerate(refs):
        step = 512 // len(piece)
        for part, ref in enumerate(piece):
            pltpu.make_async_copy(
                ref, buffer.at[slot, pl.ds(part * step, step)], sems.at[slot]
            ).start()


def wait_piece(buffer, sems, slot):
    pltpu.make_async_copy(buffer.at[slot], buffer.at[slot], sems.at[slot]).wait()


def prep_kernel(
    segments, frequency, queries, query_gain, allowed, cosine, sine, rotated, scaled, inverses
):
    lane = lax.broadcasted_iota(jnp.int32, (128, 128), 1)
    diagonal = lax.broadcasted_iota(jnp.int32, (128, 128), 0) == lane
    for i in range(4):
        first, width = SPANS[i]
        here = pl.ds(128 * i, 128)
        own = jnp.broadcast_to(segments[:, here].astype(F32), (128, 128))
        own = jnp.sum(jnp.where(diagonal, own, 0.0), axis=1, keepdims=True)
        rows = lax.broadcasted_iota(jnp.int32, (128, width), 0) + 128 * i
        columns = lax.broadcasted_iota(jnp.int32, (128, width), 1) + first
        same = own == segments[:, pl.ds(first, width)].astype(F32)
        mask = jnp.where(same & (columns <= rows), 1.0, 0.0)
        allowed[here, 0:width] = mask
        if width < 384:
            allowed[here, width:384] = jnp.zeros((128, 384 - width), F32)
        position = jnp.sum(mask, axis=1, keepdims=True) - 1.0
        angles = position * frequency[...]
        cosine[here, :] = jnp.cos(angles)
        turn = jnp.sin(angles)
        sine[here, :] = jnp.where(lane < 64, -turn, turn)

    def head(h, carry):
        columns = pl.ds(pl.multiple_of(128 * h, 128), 128)
        for i in range(4):
            here = pl.ds(128 * i, 128)
            query = queries[here, columns].astype(F32)
            inverse = lax.rsqrt(jnp.mean(query * query, axis=-1, keepdims=True) + EPS)
            unit = query * inverse
            normed = unit * query_gain[...]
            turned = normed * cosine[here, :] + pltpu.roll(normed, 64, 1) * sine[here, :]
            rotated[here, columns] = turned.astype(BF16)
            scaled[here, columns] = unit
            inverses[here, columns] = jnp.broadcast_to(inverse, (128, 128))
        return carry

    lax.fori_loop(0, 8, head, 0)


def prep(segments, queries, query_gain):
    frequency = THETA ** (-2.0 * jnp.arange(64, dtype=F32) / 128)
    frequency = jnp.concatenate([frequency, frequency])[None, :]
    return pl.pallas_call(
        prep_kernel,
        out_shape=(
            shaped((512, 384), F32), shaped((512, 128), F32), shaped((512, 128), F32),
            shaped((512, 1024)), shaped((512, 1024), F32), shaped((512, 1024), F32),
        ),
        in_specs=[VMEM_SPEC] * 4,
        out_specs=(VMEM_SPEC,) * 6,
        compiler_params=PARAMS,
        name="prep",
    )(segments, frequency, queries, query_gain[None, :])


def project_kernel(place, *refs):
    pieces, wide = refs[:6], refs[6]
    out, blocks = refs[7], refs[8:12]
    tokens, sems, block_sems = refs[12:]
    zh, c = place[3], place[4]
    load_pieces([(piece,) for piece in pieces], tokens, sems)
    stores = [
        pltpu.make_async_copy(wide.at[lax.rem(zh + r, 4)], blocks[r], block_sems.at[r])
        for r in range(4)
    ]
    for store in stores:
        store.start()
    total = None
    for slot in range(6):
        block = lax.rem(zh + (0, 0, 1, 1, 3, 3)[slot], 4)
        core = c if slot % 2 == 0 else 1 - c
        wait_piece(tokens, sems, slot)
        part = jnp.dot(
            tokens[slot],
            wide[block, pl.ds(pl.multiple_of(core * 640, 128), 640), :],
            preferred_element_type=F32,
        )
        total = part if total is None else total + part
    out[...] = total
    for store in stores:
        store.wait()


def project(place, full, weights):
    return pl.pallas_call(
        project_kernel,
        out_shape=(shaped((512, 256), F32),) + (shaped((1280, 256)),) * 4,
        in_specs=[SMEM_SPEC] + [HBM_SPEC] * 6 + [VMEM_SPEC],
        out_specs=(VMEM_SPEC,) + (HBM_SPEC,) * 4,
        scratch_shapes=[
            pltpu.VMEM((6, 512, 640), BF16),
            DMA((6,)),
            DMA((4,)),
        ],
        compiler_params=PARAMS,
        name="project",
    )(place, *full, on_chip(weights))


def weight_grad_kernel(place, *refs):
    pieces, last, grads, mine_hbm, theirs = refs[:6], refs[6:10], *refs[10:13]
    out, crossed, tokens, partial, sems, out_sems = refs[13:19]
    mine, mine_sem = refs[19:]
    zh, c = place[3], place[4]
    load_pieces([(piece,) for piece in pieces] + [last[:2], last[2:]], tokens, sems)
    copy = pltpu.make_async_copy(mine_hbm, mine, mine_sem)
    copy.start()

    def store(slot):
        turn = jnp.where(slot < 4, slot // 2, 5 - slot // 2)
        core = jnp.where(slot % 2 == 0, c, 1 - c)
        start = pl.multiple_of((2 * lax.rem(zh + turn, 4) + core) * 640, 128)
        return pltpu.make_async_copy(
            partial.at[slot], out.at[pl.ds(start, 640)], out_sems.at[slot]
        )

    def step(slot, carry):
        wait_piece(tokens, sems, slot)
        part = lax.dot_general(
            tokens[slot], grads[...], TN, preferred_element_type=F32
        )
        partial[slot] = part.astype(BF16)
        store(slot).start()
        return carry

    lax.fori_loop(0, 8, step, 0)
    copy.wait()
    crossed[...] = (mine[...] + theirs[...].astype(F32)).astype(BF16)
    for slot in range(8):
        store(slot).wait()


def weight_grad(place, full, halves, grads, mine, theirs):
    return pl.pallas_call(
        weight_grad_kernel,
        out_shape=(shaped((5120, 256)), shaped((512, 640))),
        in_specs=[SMEM_SPEC] + [HBM_SPEC] * 10 + [VMEM_SPEC, HBM_SPEC, VMEM_SPEC],
        out_specs=(HBM_SPEC, VMEM_SPEC),
        scratch_shapes=[
            pltpu.VMEM((8, 512, 640), BF16),
            pltpu.VMEM((8, 640, 256), BF16),
            DMA((8,)),
            DMA((8,)),
            pltpu.VMEM((512, 640), F32),
            DMA,
        ],
        compiler_params=PARAMS,
        name="weight_grad",
    )(place, *full, *halves, grads, mine, on_chip(theirs))


def sum_rows_kernel(place, parts, gains, keep, away):
    zl = place[2]
    for out, half in ((keep, zl), (away, 1 - zl)):
        out[160:168, 0:128] = gains[...]
        out[160:168, 128:256] = gains[...]
        rows = pl.ds(pl.multiple_of(half * 160, 32), 160)
        total = parts[0, rows].astype(F32)
        for r in range(1, 16):
            total = total + parts[r, rows].astype(F32)
        out[0:160, :] = total


def sum_rows(place, parts, gains):
    return pl.pallas_call(
        sum_rows_kernel,
        out_shape=(shaped((168, 256), F32), shaped((168, 256), F32)),
        in_specs=[SMEM_SPEC, VMEM_SPEC, VMEM_SPEC],
        out_specs=(VMEM_SPEC, VMEM_SPEC),
        compiler_params=PARAMS,
        name="sum_rows",
    )(place, on_chip(parts), gains)


def sum_last_kernel(keep, away, key_out, value_out, gains):
    total = keep[...] + away[...]
    key_out[...] = total[:160, :128]
    value_out[...] = total[:160, 128:]
    gains[...] = total[160:162, :128]


def small(kernel, outs, *operands):
    specs = [SMEM_SPEC if o.ndim == 1 else VMEM_SPEC for o in operands]
    return pl.pallas_call(
        kernel,
        out_shape=tuple(outs),
        in_specs=specs,
        out_specs=tuple([VMEM_SPEC] * len(outs)),
        compiler_params=PARAMS,
    )(*(o if o.ndim == 1 else on_chip(o) for o in operands))


def token_grad_kernel(place, *refs):
    count = len(refs) // 2 - 1
    grads, weights, (mine, theirs) = refs[:count], refs[count : 2 * count], refs[2 * count :]
    c = place[4]
    for out, core in ((theirs, 1 - c), (mine, c)):
        rows = pl.ds(pl.multiple_of(core * 640, 128), 640)
        total = None
        for grad, weight in zip(grads, weights):
            part = lax.dot_general(grad[...], weight[rows, :], NT, preferred_element_type=F32)
            total = part if total is None else total + part
        out[...] = total.astype(out.dtype)


def token_grad_of(place, grads, weights):
    return small(
        token_grad_kernel,
        [shaped((512, 640), F32), shaped((512, 640))],
        place, *grads, *weights,
    )


def attention_kernel(
    place, partial, top, bottom, top_partner, bottom_partner, opposite, rotated, scaled_in, inverses, grads_in,
    cosine, sine, allowed, query_gain, key_gain,
    context, query_grad, grads, gains_out, cross_mine, cross_theirs,
    raw, key_rot, value, key_acc, value_acc, gains,
):
    step = pl.program_id(0)
    scale = 128**-0.5

    @pl.when(step == 0)
    def _():
        core = place[4]
        mine = opposite[pl.ds(pl.multiple_of(core * 640, 128), 640), :]
        other = opposite[pl.ds(pl.multiple_of((1 - core) * 640, 128), 640), :]
        for half, (a, b) in enumerate(((top, top_partner), (bottom, bottom_partner))):
            rows = pl.ds(256 * half, 256)
            raw[rows, :] = (
                partial[rows, :]
                + jnp.dot(a[...], mine, preferred_element_type=F32)
                + jnp.dot(b[...], other, preferred_element_type=F32)
            )
        key_raw = raw[:, :128]
        inverse = lax.rsqrt(jnp.mean(key_raw * key_raw, axis=-1, keepdims=True) + EPS)
        normed = key_raw * inverse * key_gain[...]
        key_rot[...] = (normed * cosine[...] + pltpu.roll(normed, 64, 1) * sine[...]).astype(BF16)
        value[...] = raw[:, 128:].astype(BF16)
        key_acc[...] = jnp.zeros_like(key_acc)
        value_acc[...] = jnp.zeros_like(value_acc)
        gains[...] = jnp.zeros_like(gains)

    gain = query_gain[...]
    gain_sum = jnp.zeros((1, 128), F32)

    def heads(ref, rows):
        return jnp.concatenate([ref[rows, pl.ds(128 * h, 128)] for h in range(HEADS)], axis=0)

    def again(tile):
        return jnp.concatenate([tile] * HEADS, axis=0)

    for i in range(4):
        first, width = SPANS[i]
        here, span = pl.ds(128 * i, 128), pl.ds(first, width)
        query_rot, scaled = heads(rotated, here), heads(scaled_in, here)
        inverse = heads(inverses, here)
        cos, sin = again(cosine[here, :]), again(sine[here, :])
        keys, values, upstream = key_rot[span, :], value[span, :], heads(grads_in, here)
        scores = lax.dot_general(query_rot, keys, NT, preferred_element_type=F32)
        exponent = jnp.exp2(scores * (scale * LOG2E)) * again(allowed[here, pl.ds(0, width)])
        weights = exponent * (1.0 / jnp.sum(exponent, axis=-1, keepdims=True))
        rounded = weights.astype(BF16)
        mixed = jnp.dot(rounded, values, preferred_element_type=F32).astype(BF16)
        dot_grad = lax.dot_general(upstream, values, NT, preferred_element_type=F32)
        delta = jnp.sum(weights * dot_grad, axis=-1, keepdims=True)
        score_grad = (weights * (dot_grad - delta)).astype(BF16)
        value_acc[span, :] += lax.dot_general(rounded, upstream, TN, preferred_element_type=F32)
        key_acc[span, :] += lax.dot_general(score_grad, query_rot, TN, preferred_element_type=F32)
        rot_grad = jnp.dot(score_grad, keys, preferred_element_type=F32) * scale
        normed_grad = rot_grad * cos - pltpu.roll(rot_grad, 64, 1) * sin
        gain_sum += jnp.sum(normed_grad * scaled, axis=0, keepdims=True)
        weighted = gain * normed_grad
        mean = jnp.mean(scaled * weighted, axis=-1, keepdims=True)
        raw_grad = (inverse * (weighted - scaled * mean)).astype(BF16)
        for h in range(HEADS):
            context[here, pl.ds(128 * h, 128)] = mixed[128 * h : 128 * h + 128]
            query_grad[here, pl.ds(128 * h, 128)] = raw_grad[128 * h : 128 * h + 128]
    gains[0:1, :] += gain_sum

    @pl.when(step == pl.num_programs(0) - 1)
    def _():
        key_raw = raw[:, :128]
        inverse = lax.rsqrt(jnp.mean(key_raw * key_raw, axis=-1, keepdims=True) + EPS)
        scaled = key_raw * inverse
        rot_grad = key_acc[...] * scale
        normed_grad = rot_grad * cosine[...] - pltpu.roll(rot_grad, 64, 1) * sine[...]
        gains[1:2, :] = jnp.sum(normed_grad * scaled, axis=0, keepdims=True)
        weighted = key_gain[...] * normed_grad
        mean = jnp.mean(scaled * weighted, axis=-1, keepdims=True)
        grads[:, :128] = (inverse * (weighted - scaled * mean)).astype(BF16)
        grads[:, 128:] = value_acc[...].astype(BF16)
        for r in range(16):
            gains_out[r] = gains[...]
        core = place[4]
        for out, half in ((cross_theirs, 1 - core), (cross_mine, core)):
            rows = pl.ds(pl.multiple_of(half * 640, 128), 640)
            part = lax.dot_general(
                grads[...], opposite[rows, :], NT, preferred_element_type=F32
            )
            out[...] = part.astype(out.dtype)


def attention(place, partial, last, opposite, query_gain, key_gain, tables, context_grad):
    allowed, cosine, sine, *prepared = tables
    head = pl.BlockSpec((512, 128 * HEADS), lambda h: (0, h))

    def whole(*shape):
        return pl.BlockSpec(shape, lambda h: (0, 0))

    return pl.pallas_call(
        attention_kernel,
        grid=(8 // HEADS,),
        out_shape=(
            jax.ShapeDtypeStruct((512, 1024), BF16),
            jax.ShapeDtypeStruct((512, 1024), BF16),
            jax.ShapeDtypeStruct((512, 256), BF16),
            jax.ShapeDtypeStruct((16, 8, 128), F32),
            jax.ShapeDtypeStruct((512, 640), F32),
            jax.ShapeDtypeStruct((512, 640), BF16),
        ),
        in_specs=[
            SMEM_SPEC, whole(512, 256), *[VMEM_SPEC] * 4, whole(1280, 256), *[head] * 4, whole(512, 128), whole(512, 128),
            whole(512, 384), whole(1, 128), whole(1, 128),
        ],
        out_specs=(
            head, head, whole(512, 256), pl.BlockSpec((16, 8, 128), lambda h: (0, 0, 0)),
            whole(512, 640), whole(512, 640),
        ),
        scratch_shapes=[
            pltpu.VMEM((512, 256), F32),
            pltpu.VMEM((512, 128), BF16),
            pltpu.VMEM((512, 128), BF16),
            pltpu.VMEM((512, 128), F32),
            pltpu.VMEM((512, 128), F32),
            pltpu.VMEM((8, 128), F32),
        ],
        compiler_params=pltpu.CompilerParams(
            vmem_limit_bytes=60 * 1024 * 1024, dimension_semantics=("arbitrary",)
        ),
        name="attention",
    )(
        place, partial, *map(on_chip, last), opposite, *prepared, context_grad, cosine, sine,
        allowed, query_gain[None, :], key_gain[None, :],
    )


def local(
    tokens, queries, key_weight, value_weight, query_gain, key_gain, segment_ids, context_grad
):
    node, lane = lax.axis_index("node"), lax.axis_index("local")
    y, x, zl, zh, c = node // 8, node // 2 % 4, node % 2, lane // 2, lane % 2
    place = jnp.stack([y, x, zl, zh, c]).astype(jnp.int32)

    stacked = jnp.concatenate([key_weight, value_weight], axis=1)
    other = shift(stacked, dzl=1)
    first = (jnp.arange(2) == zl)[None, :, None, None]
    pairs = jnp.where(first, stacked[None, None], other[None, None])
    pairs = jnp.broadcast_to(pairs, (16, 2, 160, 256)).reshape(16, 320, 256)
    columns = swap(pairs).reshape(4, 1280, 256)
    before, after = shift(tokens, dzh=1), shift(tokens, dzh=-1)
    opposite = [shift(before[:256], dzh=1), shift(after[256:], dzh=-1)]
    full = [tokens, shift(tokens, dc=1), after, shift(after, dc=1)]
    full += [before, shift(before, dc=1)]
    opposite += [shift(opposite[0], dc=1), shift(opposite[1], dc=1)]
    tables = prep(segment_ids, queries, query_gain)
    partial, *blocks = project(place, full, columns)
    rows_after = shift(blocks[3], dzh=-1)
    rows_before = shift(blocks[1], dzh=1)
    context, query_grad, grads, gains, mine, theirs = attention(
        place, partial, opposite, blocks[2], query_gain, key_gain, tables,
        context_grad,
    )

    weight_part, crossed = weight_grad(place, full, opposite, grads, mine, shift(theirs, dc=1))
    gains = jnp.sum(swap(gains), axis=0)
    gains += send(gains, lambda y, x, zl, zh, c: (y, x, zl, zh ^ 1, c))
    gains += send(gains, lambda y, x, zl, zh, c: (y, x, zl, zh ^ 2, c))
    gains += shift(gains, dc=1)
    weight_part = swap(weight_part.reshape(16, 320, 256))
    grads_after = shift(grads, dzh=-1)
    grads_before = shift(grads, dzh=1)
    crossed = shift(crossed, dzh=2)
    mine, theirs = token_grad_of(
        place, [grads, grads_after, grads_before], [blocks[0], rows_after, rows_before]
    )
    token_grad = mine + shift(theirs, dc=1).astype(F32) + crossed.astype(F32)
    keep, away = sum_rows(place, weight_part, gains)
    key_weight_grad, value_weight_grad, gains = small(
        sum_last_kernel,
        [shaped((160, 128), F32)] * 2 + [shaped((2, 128), F32)],
        keep, shift(away, dzl=1),
    )
    return (
        context,
        token_grad.astype(BF16),
        query_grad,
        key_weight_grad,
        value_weight_grad,
        gains,
    )


def solution(mesh):
    in_specs = (
        P("node", "local"),
        P("node", "local"),
        P("node", "local"),
        P("node", "local"),
        P(),
        P(),
        P("node", None),
        P("node", "local"),
    )
    out_specs = (
        P("node", "local"),
        P("node", "local"),
        P("node", "local"),
        P("node", "local"),
        P("node", "local"),
        P(),
    )
    return jax.shard_map(local, mesh=mesh, in_specs=in_specs, out_specs=out_specs, check_vma=False)
```
